128 devices in a mesh: bond: 32 (over y, x, core), mpo: 4 (over z).
Axes of the slice: x: 4, y: 4, z: 4, core: 2. Of those that a mesh axis runs over, the one named last changes fastest.
Arguments:
- carried: bfloat16 [198, 8192], P(None, 'bond'), may hold values from -6 to 6
- site_tensors: bfloat16 [2, 8192, 4, 8192], P(None, 'bond', 'mpo'), may hold values from -0.125 to 0.125
- operator_tensors: bfloat16 [2, 4, 66, 264], replicated, may hold values from -0.375 to 0.375
- rotation: bfloat16 [2, 8192, 4, 8192], P(None, 'bond', 'mpo'), may hold values from -0.125 to 0.125
- kept_columns: int32 [2, 8192], replicated, may hold values from 0 to 32767, as said below
Outputs:
- rotated_state: bfloat16 [198, 8192], P(None, 'bond')
- truncation_gram: float32 [2, 198, 198], replicated
The draws below stay inside these ranges and needn't reach their ends.
Inputs may be any that keep to these rules, and one draw needn't show every extreme that they name: `kept_columns`: each row holds 8192 distinct values; value r * 4 + t names right-bond index r and physical index t.
All inputs are finite; a program needn't handle non-finite values.
Results may differ from the reference program's by a relative error of at most 0.035.
Values may be sent and summed in bfloat16 or wider, within the bound.
No kernel may reach another device: no remote copies, remote signals or barrier semaphores. Data moves between devices by JAX's collectives and lax.ppermute only.
A program may use at most 128 MiB of HBM per device.

```python
import jax
import jax.numpy as jnp
from jax import lax

BOND_DIM = 8192
PHYSICAL = 4
MPO_BOND = 66
LEFT_ROWS = 3
SITE_COUNT = 2
ROW_TOTAL = 198
N_BOND = 32


def draw_kept_columns(key, part):
    listed = []
    for position in range(SITE_COUNT):
        shuffled = jax.random.permutation(jax.random.fold_in(key, 11 + position), PHYSICAL * BOND_DIM)
        listed.append(shuffled[:BOND_DIM].astype(jnp.int32))
    return jnp.stack(listed)


def raised(drawn, stream_key, source, target, parts, factor):
    owner, partner = [(jnp.arange(drawn.shape[dim]) // (drawn.shape[dim] // parts)).reshape([-1 if axis == dim else 1 for axis in range(drawn.ndim)]) for dim in (source, target)]
    chosen = jax.random.permutation(stream_key, parts)[partner]
    strong = (owner == chosen) | (owner == (partner + parts // 2) % parts)
    return jnp.where(strong, factor * drawn, drawn)


def steps_of(own_key, extent, cuts, smallest, largest):
    def one(dim, parts):
        steps = jax.random.uniform(jax.random.fold_in(jax.random.fold_in(own_key, 6), dim), (parts,), jnp.float32, smallest / len(cuts), largest / len(cuts))
        return jnp.repeat(jnp.exp(steps), extent[dim] // parts).reshape((-1,) + (1,) * (len(extent) - dim - 1))

    gain = one(*cuts[0])
    for cut in cuts[1:]:
        gain = gain * one(*cut)
    return gain


def normal_values(stream_key, extent, scale, limit, cuts=(), held_as=jnp.bfloat16):
    gain = steps_of(stream_key, extent, cuts, -0.22, 0.18) if cuts else 1.0
    entries = jax.random.normal(stream_key, extent, jnp.float32) * scale * gain
    return jnp.minimum(jnp.maximum(entries, -limit), limit).astype(held_as)


def noise_with(rng, dims, scale, limit, pieces, heavy, held_as=jnp.bfloat16):
    array = scale * jax.random.normal(rng, dims, jnp.float32)
    if pieces:
        array = array * steps_of(rng, dims, pieces, -0.22, 0.18)
    return jnp.clip(raised(array, jax.random.fold_in(rng, 3), *heavy), -limit, limit).astype(held_as)


def setup_inputs(seed: int = 0) -> dict:
    key_of = jax.random.split(jax.random.key(seed), 6)
    carried = normal_values(key_of[0], (ROW_TOTAL, BOND_DIM), 1.0, 6.0, ((1, 32),))
    site_tensors = noise_with(key_of[1], (SITE_COUNT, BOND_DIM, PHYSICAL, BOND_DIM), BOND_DIM ** -0.5, 0.125, ((1, 32), (2, 4)), (1, 3, 32, 2.75))
    operator_tensors = normal_values(key_of[2], (SITE_COUNT, PHYSICAL, MPO_BOND, PHYSICAL * MPO_BOND), (PHYSICAL * MPO_BOND) ** -0.5, 0.375)
    rotation = noise_with(key_of[3], (SITE_COUNT, BOND_DIM, PHYSICAL, BOND_DIM), BOND_DIM ** -0.5, 0.125, ((1, 32), (2, 4)), (1, 3, 32, 2.75))
    kept_columns = draw_kept_columns(jax.random.fold_in(key_of[5], 71), 0)
    return {"carried": carried, "site_tensors": site_tensors, "operator_tensors": operator_tensors, "rotation": rotation, "kept_columns": kept_columns}


def reference(carried, site_tensors, operator_tensors, rotation, kept_columns):
    row_count = carried.shape[0]
    width = carried.shape[1]
    block_width = width // N_BOND
    state = carried
    gram_list = []
    for position in range(SITE_COUNT):
        tensor = site_tensors[position].reshape(width, PHYSICAL * width)

        def accumulate(running, number, state=state, tensor=tensor):
            offset = (number * block_width).astype(jnp.int32)
            left_block = lax.dynamic_slice_in_dim(state, offset, block_width, 1)
            right_block = lax.dynamic_slice_in_dim(tensor, offset, block_width, 0)
            rounded = jnp.dot(left_block, right_block, preferred_element_type=jnp.float32).astype(jnp.bfloat16)
            rounded = lax.optimization_barrier(rounded)
            return running + rounded.astype(jnp.float32), None

        summed, _ = lax.scan(accumulate, jnp.zeros((row_count, PHYSICAL * width), jnp.float32),
                             jnp.arange(N_BOND, dtype=jnp.int32))
        contracted = summed.astype(jnp.bfloat16).reshape(LEFT_ROWS, MPO_BOND, PHYSICAL, width)
        mixed_rows = jnp.einsum('lasr,sac->lcr', contracted.astype(jnp.float32),
                                operator_tensors[position].astype(jnp.float32),
                                precision=lax.Precision.HIGHEST)
        mixed_rows = mixed_rows.reshape(LEFT_ROWS, PHYSICAL, MPO_BOND, width)
        chosen = jnp.zeros((PHYSICAL * width,), jnp.float32).at[kept_columns[position]].set(1.0)
        chosen = chosen.reshape(width, PHYSICAL)
        kept_rows = (mixed_rows * chosen.T[None, :, None, :]).astype(jnp.bfloat16)
        kept_float = kept_rows.astype(jnp.float32)
        gram_matrix = jnp.einsum('ltar,mtbr->lamb', kept_float, kept_float,
                                 precision=lax.Precision.HIGHEST).reshape(row_count, row_count) / width
        gram_list.append(gram_matrix)
        flattened = kept_rows.transpose(0, 2, 3, 1).reshape(row_count, width * PHYSICAL)
        rotated = jnp.dot(flattened, rotation[position].reshape(width * PHYSICAL, width),
                          preferred_element_type=jnp.float32)
        state = rotated.astype(jnp.bfloat16)
    return state, jnp.stack(gram_list)
```

```python
import functools

import jax
import jax.numpy as jnp
from jax import lax
from jax.experimental import pallas as pl
from jax.experimental.pallas import tpu as pltpu
from jax.sharding import Mesh
from jax.sharding import PartitionSpec as P

BOND_DIM = 8192
PHYSICAL = 4
MPO_BOND = 66
LEFT_ROWS = 3
SITE_COUNT = 2
ROWS = LEFT_ROWS * MPO_BOND
BOND = ("y", "x", "core")
RING = 4
BLOCK = 256
F32 = jnp.float32
BF16 = jnp.bfloat16


def summed(terms):
    total = terms[0].astype(F32)
    for term in terms[1:]:
        total = total + term.astype(F32)
    return total


def chip_device(y, x, core):
    return (y % RING * RING + x % RING) * 2 + core


def shifts(step, x_core):
    pairs = []
    for y in range(RING):
        for x in range(RING):
            pairs.append((chip_device(y, x, x_core), chip_device(y, x + step, x_core)))
            other = 1 - x_core
            pairs.append((chip_device(y, x, other), chip_device(y + step, x, other)))
    return pairs


def ring_shift(step):
    return [(i, (i + step) % RING) for i in range(RING)]


def swap_cores(array):
    return lax.ppermute(array, "core", [(0, 1), (1, 0)])


def block_order(core):
    y, x = lax.axis_index("y"), lax.axis_index("x")
    far = jnp.repeat(jnp.arange(RING), RING)
    near = jnp.tile(jnp.arange(RING), RING)
    dy = jnp.where(core == 0, near, far)
    dx = jnp.where(core == 0, far, near)
    return (((y + dy) % RING * RING + (x + dx) % RING) * 2 + core).astype(jnp.int32)


def column_copy(site, order, weights, tiles, sems, i):
    first = pl.multiple_of(order[i] * BLOCK, BLOCK)
    source = weights.at[pl.ds(site * BLOCK, BLOCK), pl.ds(first, BLOCK)]
    return pltpu.make_async_copy(source, tiles.at[i], sems.at[i])


def start_columns(site, order, weights, tiles, sems):
    @pl.loop(0, RING * RING)
    def _(i):
        column_copy(site, order, weights, tiles, sems, i).start()

    return functools.partial(column_copy, site, order, weights, tiles, sems)


def multiply_columns(left, copies, tiles, outs):
    for d, out in enumerate(outs):

        @pl.loop(0, RING)
        def _(e, d=d, out=out):
            i = d * RING + e
            copies(i).wait()
            product = jnp.dot(left[...], tiles[i], preferred_element_type=F32)
            out[e] = product.astype(BF16)


def plain_kernel(site, order, left, weights, *rest):
    outs, (tiles, sems) = rest[:RING], rest[RING:]
    copies = start_columns(site, order, weights, tiles, sems)
    multiply_columns(left, copies, tiles, outs)


def sum_kernel(site, order, a, b, c, d, weights, state, *rest):
    outs, (tiles, sems) = rest[:RING], rest[RING:]
    copies = start_columns(site, order, weights, tiles, sems)
    state[...] = summed([a[...], b[...], c[...], d[...]]).astype(BF16)
    multiply_columns(state, copies, tiles, outs)


def mix_kernel(site, order, a, b, c, d, mixing, chosen, weights, kept, *rest):
    outs, (tiles, sems) = rest[:RING], rest[RING:]
    copies = start_columns(site, order, weights, tiles, sems)
    mixed = jnp.zeros((ROWS, BLOCK), F32)
    for i, part in enumerate((a, b, c, d)):
        mixed = mixed + jnp.dot(mixing[i], part[...], preferred_element_type=F32)
    kept[...] = (mixed * chosen[...]).astype(BF16)
    multiply_columns(kept, copies, tiles, outs)


def gram_kernel(site, order, left, weights, *rest):
    outs, gram, (tiles, sems) = rest[:RING], rest[RING], rest[RING + 1 :]
    copies = start_columns(site, order, weights, tiles, sems)
    multiply_columns(left, copies, tiles, outs)
    kept = left[...]
    whole = lax.dot_general(kept, kept, (((1,), (1,)), ((), ())), preferred_element_type=F32)
    gram[...] = (whole * (1.0 / BOND_DIM)).astype(BF16)


VMEM = pl.BlockSpec(memory_space=pltpu.VMEM)
PIECES = [jax.ShapeDtypeStruct((RING, ROWS, BLOCK), BF16)] * RING
SQUARE = jax.ShapeDtypeStruct((ROWS, ROWS), BF16)
TALL = jax.ShapeDtypeStruct((ROWS, BLOCK), BF16)


def call(kernel, site, order, operands, weights, before=(), after=()):
    shapes = [*before, *PIECES, *after]
    flops = 2 * ROWS * BLOCK * BLOCK * RING * RING
    return pl.pallas_call(
        functools.partial(kernel, site),
        out_shape=shapes,
        in_specs=[pl.BlockSpec(memory_space=pltpu.SMEM)]
        + [VMEM] * len(operands)
        + [pl.BlockSpec(memory_space=pl.ANY)],
        out_specs=[VMEM] * len(shapes),
        scratch_shapes=[
            pltpu.VMEM((RING * RING, BLOCK, BLOCK), BF16),
            pltpu.SemaphoreType.DMA((RING * RING,)),
        ],
        compiler_params=pltpu.CompilerParams(vmem_limit_bytes=24 * 2**20),
        cost_estimate=pl.CostEstimate(
            flops=flops, bytes_accessed=4 * 2**20, transcendentals=0
        ),
    )(order, *operands, weights)


def scattered(theirs, ours):
    arrived = [swap_cores(theirs[d]) for d in (2, 1, 3, 0)]
    mine = {d: summed([ours[d], got]).astype(BF16) for d, got in zip((2, 1, 3, 0), arrived)}
    got = [lax.ppermute(mine[d], BOND, shifts(d, 0)) for d in (2, 1, 3)]
    near = summed([mine[0], *got]).astype(BF16)
    got = [lax.ppermute(near[e], BOND, shifts(e, 1)) for e in (2, 1, 3)]
    return summed([near[0], *got]).astype(BF16)


def along_z(array):
    return [array] + [lax.ppermute(array, "z", ring_shift(d)) for d in (1, 2, 3)]


def mixing_weights(operator_tensors):
    z = lax.axis_index("z")
    turned = jnp.stack(
        [
            lax.dynamic_index_in_dim(operator_tensors, (z - d) % RING, 1, keepdims=False)
            for d in range(RING)
        ],
        1,
    )
    row = jnp.arange(ROWS)
    pick = (z * MPO_BOND + row[:, None] % MPO_BOND == jnp.arange(PHYSICAL * MPO_BOND)).astype(BF16)
    spread = (jnp.arange(MPO_BOND)[:, None] == row[None] % MPO_BOND).astype(BF16)
    narrow = jnp.einsum("xc,kdac->kdxa", pick, turned, preferred_element_type=F32).astype(BF16)
    wide = jnp.einsum("kdxa,aw->kdxw", narrow, spread, preferred_element_type=F32)
    same = row[:, None] // MPO_BOND == row[None] // MPO_BOND
    return jnp.where(same, wide, 0.0).astype(BF16)


def chosen_columns(kept_columns):
    first = lax.axis_index(BOND) * BLOCK * PHYSICAL
    place = kept_columns - first
    here = (place >= 0) & (place < BLOCK * PHYSICAL) & (place % PHYSICAL == lax.axis_index("z"))
    column = place // PHYSICAL
    digits = jnp.arange(16)[None, :, None]
    high = ((column // 16)[:, None] == digits) & here[:, None]
    low = (column % 16)[:, None] == digits
    counts = jnp.einsum(
        "khn,kln->khl", high.astype(BF16), low.astype(BF16), preferred_element_type=F32
    )
    return (counts > 0.5).astype(F32).reshape(SITE_COUNT, 1, BLOCK)


def total_grams(grams):
    core = lax.axis_index("core")
    own = jnp.where(core == 0, grams[0], grams[1])
    total = summed([own, swap_cores(jnp.where(core == 0, grams[1], grams[0]))]).astype(BF16)
    for axis in ("z", "x", "y"):
        got = [lax.ppermute(total, axis, ring_shift(d)) for d in (1, 2, 3)]
        total = summed([total, *got])
        if axis != "y":
            total = total.astype(BF16)
    other = swap_cores(total)
    return jnp.stack([jnp.where(core == 0, total, other), jnp.where(core == 0, other, total)])


def on_device(carried, site_tensors, operator_tensors, rotation, kept_columns):
    core = lax.axis_index("core")
    their_order, our_order = block_order(1 - core), block_order(core)
    tensors = site_tensors.reshape(SITE_COUNT * BLOCK, BOND_DIM)
    turns = rotation.reshape(SITE_COUNT * BLOCK, BOND_DIM)
    mixing = mixing_weights(operator_tensors)
    chosen = chosen_columns(kept_columns)
    grams, parts = [], None
    for site in range(SITE_COUNT):
        if parts is None:
            state = carried
            theirs = call(plain_kernel, site, their_order, [state], tensors)
        else:
            state, *theirs = call(sum_kernel, site, their_order, parts, tensors, before=[TALL])
        ours = call(plain_kernel, site, our_order, [state], tensors)
        parts = along_z(scattered(theirs, ours))
        kept, *theirs = call(
            mix_kernel, site, their_order, [*parts, mixing[site], chosen[site]], turns, before=[TALL]
        )
        *ours, gram = call(gram_kernel, site, our_order, [kept], turns, after=[SQUARE])
        grams.append(gram)
        parts = along_z(scattered(theirs, ours))
    return summed(parts).astype(BF16), total_grams(grams)


def solution(mesh):
    finer = Mesh(mesh.devices.reshape(RING, RING, 2, mesh.shape["mpo"]), (*BOND, "z"))
    placed = (P(None, BOND), P(None, BOND, "z", None), P(), P(None, BOND, "z", None), P())
    return jax.shard_map(
        on_device, mesh=finer, in_specs=placed, out_specs=(P(None, BOND), P()), check_vma=False
    )
```

```python
import functools

import jax
import jax.numpy as jnp
from jax import lax
from jax.experimental import pallas as pl
from jax.experimental.pallas import tpu as pltpu
from jax.sharding import Mesh
from jax.sharding import PartitionSpec as P

BOND_DIM = 8192
PHYSICAL = 4
MPO_BOND = 66
LEFT_ROWS = 3
SITE_COUNT = 2
ROWS = LEFT_ROWS * MPO_BOND
BOND = ("y", "x", "core")
RING = 4
BLOCK = 256
SENT = (2, 1, 3, 0)
F32 = jnp.float32
BF16 = jnp.bfloat16


def summed(terms):
    total = terms[0].astype(F32)
    for term in terms[1:]:
        total = total + term.astype(F32)
    return total


def chip_device(y, x, core):
    return (y % RING * RING + x % RING) * 2 + core


def shifts(step, x_core):
    pairs = []
    for y in range(RING):
        for x in range(RING):
            pairs.append((chip_device(y, x, x_core), chip_device(y, x + step, x_core)))
            other = 1 - x_core
            pairs.append((chip_device(y, x, other), chip_device(y + step, x, other)))
    return pairs


def ring_shift(step):
    return [(i, (i + step) % RING) for i in range(RING)]


def swap_cores(array):
    return lax.ppermute(array, "core", [(0, 1), (1, 0)])


def block_order(core):
    y, x = lax.axis_index("y"), lax.axis_index("x")
    far = jnp.repeat(jnp.arange(RING), RING)
    near = jnp.tile(jnp.arange(RING), RING)
    dy = jnp.where(core == 0, near, far)
    dx = jnp.where(core == 0, far, near)
    return (((y + dy) % RING * RING + (x + dx) % RING) * 2 + core).astype(jnp.int32)


def start_columns(site, order, weights, tiles, sems):
    copies = []
    for i in range(RING * RING):
        first = pl.multiple_of(order[i] * BLOCK, BLOCK)
        source = weights.at[pl.ds(site * BLOCK, BLOCK), pl.ds(first, BLOCK)]
        target = tiles.at[:, pl.ds(i * BLOCK, BLOCK)]
        copies.append(pltpu.make_async_copy(source, target, sems.at[i]))
        copies[-1].start()
    return copies


def multiply_columns(left, copies, tiles, outs):
    width = RING * BLOCK
    for d in SENT:
        for copy in copies[d * RING : (d + 1) * RING]:
            copy.wait()
        columns = tiles[:, d * width : (d + 1) * width]
        product = jnp.dot(left[...], columns, preferred_element_type=F32).astype(BF16)
        for e in range(RING):
            outs[d][e] = product[:, e * BLOCK : (e + 1) * BLOCK]


def plain_kernel(site, order, left, weights, *rest):
    outs, (tiles, sems) = rest[:RING], rest[RING:]
    copies = start_columns(site, order, weights, tiles, sems)
    multiply_columns(left, copies, tiles, outs)


def sum_kernel(site, order, a, b, c, d, weights, state, *rest):
    outs, (tiles, sems) = rest[:RING], rest[RING:]
    copies = start_columns(site, order, weights, tiles, sems)
    state[...] = summed([a[...], b[...], c[...], d[...]]).astype(BF16)
    multiply_columns(state, copies, tiles, outs)


def mix_kernel(site, order, a, b, c, d, mixing, chosen, weights, kept, *rest):
    outs, (tiles, sems) = rest[:RING], rest[RING:]
    copies = start_columns(site, order, weights, tiles, sems)
    mixed = jnp.zeros((ROWS, BLOCK), F32)
    for i, part in enumerate((a, b, c, d)):
        mixed = mixed + jnp.dot(mixing[i], part[...], preferred_element_type=F32)
    kept[...] = (mixed * chosen[...]).astype(BF16)
    multiply_columns(kept, copies, tiles, outs)


def gram_kernel(site, order, left, weights, *rest):
    outs, gram, (tiles, sems) = rest[:RING], rest[RING], rest[RING + 1 :]
    copies = start_columns(site, order, weights, tiles, sems)
    multiply_columns(left, copies, tiles, outs)
    kept = left[...]
    whole = lax.dot_general(kept, kept, (((1,), (1,)), ((), ())), preferred_element_type=F32)
    gram[...] = (whole * (1.0 / BOND_DIM)).astype(BF16)


VMEM = pl.BlockSpec(memory_space=pltpu.VMEM)
PIECES = [jax.ShapeDtypeStruct((RING, ROWS, BLOCK), BF16)] * RING
SQUARE = jax.ShapeDtypeStruct((ROWS, ROWS), BF16)
TALL = jax.ShapeDtypeStruct((ROWS, BLOCK), BF16)


def call(kernel, site, order, operands, weights, before=(), after=()):
    shapes = [*before, *PIECES, *after]
    flops = 2 * ROWS * BLOCK * BLOCK * RING * RING
    return pl.pallas_call(
        functools.partial(kernel, site),
        out_shape=shapes,
        in_specs=[pl.BlockSpec(memory_space=pltpu.SMEM)]
        + [VMEM] * len(operands)
        + [pl.BlockSpec(memory_space=pltpu.HBM)],
        out_specs=[VMEM] * len(shapes),
        scratch_shapes=[
            pltpu.VMEM((BLOCK, RING * RING * BLOCK), BF16),
            pltpu.SemaphoreType.DMA((RING * RING,)),
        ],
        compiler_params=pltpu.CompilerParams(vmem_limit_bytes=48 * 2**20),
        cost_estimate=pl.CostEstimate(
            flops=flops, bytes_accessed=4 * 2**20, transcendentals=0
        ),
    )(order, *operands, weights)


def scattered(theirs, ours, extra=None):
    arrived = [swap_cores(theirs[d]) for d in SENT]
    mine = {d: summed([ours[d], got]).astype(BF16) for d, got in zip(SENT, arrived)}
    if extra is not None:
        mine = {d: jnp.concatenate([piece, extra[None]]) for d, piece in mine.items()}
    got = [lax.ppermute(mine[d], BOND, shifts(d, 0)) for d in (2, 1, 3)]
    near = summed([mine[0], *got]).astype(BF16)
    pieces = [near[e] for e in range(RING)]
    if extra is not None:
        pieces = [jnp.stack([piece, near[RING]]) for piece in pieces]
    got = [lax.ppermute(pieces[e], BOND, shifts(e, 1)) for e in (2, 1, 3)]
    return summed([pieces[0], *got]).astype(BF16)


def along_z(array):
    return [array] + [lax.ppermute(array, "z", ring_shift(d)) for d in (1, 2, 3)]


def mixing_kernel(z, operator_tensors, mixing):
    def iota(shape, dim):
        return lax.broadcasted_iota(jnp.int32, shape, dim)

    wide, tall = (ROWS, PHYSICAL * MPO_BOND), (MPO_BOND, ROWS)
    first = z[0] * MPO_BOND
    pick = (iota(wide, 1) == first + lax.rem(iota(wide, 0), MPO_BOND)).astype(BF16)
    spread = (iota(tall, 0) == lax.rem(iota(tall, 1), MPO_BOND)).astype(BF16)
    square = (ROWS, ROWS)
    same = lax.div(iota(square, 0), MPO_BOND) == lax.div(iota(square, 1), MPO_BOND)
    for site in range(SITE_COUNT):
        for d in range(RING):
            weights = operator_tensors[site, lax.rem(z[0] + RING - d, RING)]
            narrow = lax.dot_general(
                pick, weights, (((1,), (1,)), ((), ())), preferred_element_type=F32
            ).astype(BF16)
            full = jnp.dot(narrow, spread, preferred_element_type=F32)
            mixing[site, d] = jnp.where(same, full, 0.0).astype(BF16)


def mixing_weights(operator_tensors):
    return pl.pallas_call(
        mixing_kernel,
        out_shape=jax.ShapeDtypeStruct((SITE_COUNT, RING, ROWS, ROWS), BF16),
        in_specs=[pl.BlockSpec(memory_space=pltpu.SMEM), VMEM],
        out_specs=VMEM,
        compiler_params=pltpu.CompilerParams(vmem_limit_bytes=8 * 2**20),
        cost_estimate=pl.CostEstimate(flops=10**9, bytes_accessed=10**6, transcendentals=0),
    )(lax.axis_index("z").astype(jnp.int32)[None], operator_tensors)


def chosen_columns(kept_columns):
    first = lax.axis_index(BOND) * BLOCK * PHYSICAL
    place = kept_columns - first
    here = (place >= 0) & (place < BLOCK * PHYSICAL) & (place % PHYSICAL == lax.axis_index("z"))
    column = place // PHYSICAL
    digits = jnp.arange(16)[None, :, None]
    high = ((column // 16)[:, None] == digits) & here[:, None]
    low = (column % 16)[:, None] == digits
    counts = jnp.einsum(
        "khn,kln->khl", high.astype(BF16), low.astype(BF16), preferred_element_type=F32
    )
    return (counts > 0.5).astype(F32).reshape(SITE_COUNT, 1, BLOCK)


def chip_gram(grams):
    first = lax.axis_index("core") == 0
    got = swap_cores(jnp.where(first, grams[1], grams[0]))
    total = summed([jnp.where(first, grams[0], grams[1]), got]).astype(BF16)
    return jnp.pad(total, ((0, 0), (0, BLOCK - ROWS)))


def both_grams(total):
    own = total[:, :ROWS]
    other = swap_cores(own)
    first = lax.axis_index("core") == 0
    return jnp.stack([jnp.where(first, own, other), jnp.where(first, other, own)])


def on_device(carried, site_tensors, operator_tensors, rotation, kept_columns):
    core = lax.axis_index("core")
    their_order, our_order = block_order(1 - core), block_order(core)
    tensors = site_tensors.reshape(SITE_COUNT * BLOCK, BOND_DIM)
    turns = rotation.reshape(SITE_COUNT * BLOCK, BOND_DIM)
    mixing = mixing_weights(operator_tensors)
    chosen = chosen_columns(kept_columns)
    grams, parts = [], None
    for site in range(SITE_COUNT):
        if parts is None:
            state = carried
            theirs = call(plain_kernel, site, their_order, [state], tensors)
        else:
            state, *theirs = call(sum_kernel, site, their_order, parts, tensors, before=[TALL])
        ours = call(plain_kernel, site, our_order, [state], tensors)
        parts = along_z(scattered(theirs, ours))
        kept, *theirs = call(
            mix_kernel, site, their_order, [*parts, mixing[site], chosen[site]], turns, before=[TALL]
        )
        *ours, gram = call(gram_kernel, site, our_order, [kept], turns, after=[SQUARE])
        grams.append(gram)
        last = site == SITE_COUNT - 1
        parts = along_z(scattered(theirs, ours, chip_gram(grams) if last else None))
    total = summed(parts)
    return total[0].astype(BF16), both_grams(total[1])


def solution(mesh):
    finer = Mesh(mesh.devices.reshape(RING, RING, 2, mesh.shape["mpo"]), (*BOND, "z"))
    placed = (P(None, BOND), P(None, BOND, "z", None), P(), P(None, BOND, "z", None), P())
    return jax.shard_map(
        on_device, mesh=finer, in_specs=placed, out_specs=(P(None, BOND), P()), check_vma=False
    )
```

```python
import functools

import jax
import jax.numpy as jnp
from jax import lax
from jax.experimental import pallas as pl
from jax.experimental.pallas import tpu as pltpu
from jax.sharding import Mesh
from jax.sharding import PartitionSpec as P

BOND_DIM = 8192
PHYSICAL = 4
MPO_BOND = 66
LEFT_ROWS = 3
SITE_COUNT = 2
ROWS = LEFT_ROWS * MPO_BOND
BOND = ("y", "x", "core")
RING = 4
BLOCK = 256
SENT = (2, 1, 3, 0)
LOADS = 8
LOAD_GRANT = 48 * 2**20
GRANT = 16 * 2**20
F32 = jnp.float32
BF16 = jnp.bfloat16


def summed(terms):
    total = terms[0].astype(F32)
    for term in terms[1:]:
        total = total + term.astype(F32)
    return total


def chip_device(y, x, core):
    return (y % RING * RING + x % RING) * 2 + core


def shifts(step, x_core):
    pairs = []
    for y in range(RING):
        for x in range(RING):
            pairs.append((chip_device(y, x, x_core), chip_device(y, x + step, x_core)))
            other = 1 - x_core
            pairs.append((chip_device(y, x, other), chip_device(y + step, x, other)))
    return pairs


def ring_shift(step):
    return [(i, (i + step) % RING) for i in range(RING)]


def swap_cores(array):
    return lax.ppermute(array, "core", [(0, 1), (1, 0)])


def block_order(core):
    y, x = lax.axis_index("y"), lax.axis_index("x")
    far = jnp.repeat(jnp.arange(RING), RING)
    near = jnp.tile(jnp.arange(RING), RING)
    dy = jnp.where(core == 0, near, far)
    dx = jnp.where(core == 0, far, near)
    return (((y + dy) % RING * RING + (x + dx) % RING) * 2 + core).astype(jnp.int32)


def load_kernel(site, after, weights, loaded, sems):
    rows = BLOCK // LOADS
    copies = []
    for i in range(LOADS):
        source = weights.at[pl.ds(site * BLOCK + i * rows, rows), :]
        copies.append(
            pltpu.make_async_copy(source, loaded.at[pl.ds(i * rows, rows), :], sems.at[i])
        )
        copies[-1].start()
    for copy in copies:
        copy.wait()


def load(site, weights, after):
    return pl.pallas_call(
        functools.partial(load_kernel, site),
        out_shape=jax.ShapeDtypeStruct((BLOCK, BOND_DIM), BF16),
        in_specs=[pl.BlockSpec(memory_space=pl.ANY)] * 2,
        out_specs=VMEM,
        scratch_shapes=[pltpu.SemaphoreType.DMA((LOADS,))],
        compiler_params=pltpu.CompilerParams(vmem_limit_bytes=LOAD_GRANT),
        cost_estimate=pl.CostEstimate(flops=0, bytes_accessed=4 * 2**20, transcendentals=0),
    )(after, weights)


def multiply_kernel(prepare, given, order, *refs):
    operands, weights, refs = refs[:given], refs[given], refs[given + 1 :]
    if prepare is None:
        left, outs = operands[0], refs
    else:
        left, outs = refs[0], refs[1:]
        left[...] = prepare(*operands).astype(BF16)
    for group in range(len(outs) // RING):
        for d in SENT:
            for e in range(RING):
                number = order[(group * RING + d) * RING + e]
                columns = weights[:, pl.ds(pl.multiple_of(number * BLOCK, BLOCK), BLOCK)]
                product = jnp.dot(left[...], columns, preferred_element_type=F32)
                outs[group * RING + d][e] = product.astype(BF16)


def direct_kernel(site, order, left, weights, *rest):
    outs, (tiles, sems) = rest[:RING], rest[RING:]
    width = RING * BLOCK
    copies = []
    for i in range(RING**2):
        first = pl.multiple_of(order[i] * BLOCK, BLOCK)
        source = weights.at[pl.ds(site * BLOCK, BLOCK), pl.ds(first, BLOCK)]
        target = tiles.at[:, pl.ds(i * BLOCK, BLOCK)]
        copies.append(pltpu.make_async_copy(source, target, sems.at[i]))
    for d in SENT:
        for e in range(RING):
            copies[d * RING + e].start()
    for d in SENT:
        for e in range(RING):
            copies[d * RING + e].wait()
        columns = tiles[:, d * width : (d + 1) * width]
        product = jnp.dot(left[...], columns, preferred_element_type=F32).astype(BF16)
        for e in range(RING):
            outs[d][e] = product[:, e * BLOCK : (e + 1) * BLOCK]


def multiply_direct(site, left, order, weights):
    return pl.pallas_call(
        functools.partial(direct_kernel, site),
        out_shape=[jax.ShapeDtypeStruct((RING, ROWS, BLOCK), BF16)] * RING,
        in_specs=[pl.BlockSpec(memory_space=pltpu.SMEM), VMEM, pl.BlockSpec(memory_space=pl.ANY)],
        out_specs=[VMEM] * RING,
        scratch_shapes=[
            pltpu.VMEM((BLOCK, RING**2 * BLOCK), BF16),
            pltpu.SemaphoreType.DMA((RING**2,)),
        ],
        compiler_params=pltpu.CompilerParams(vmem_limit_bytes=LOAD_GRANT),
        cost_estimate=pl.CostEstimate(flops=10**9, bytes_accessed=2**22, transcendentals=0),
    )(order, left, weights)


def gram_kernel(*refs):
    kept, gram = refs[-2:]
    whole = lax.dot_general(
        kept[...], kept[...], (((1,), (1,)), ((), ())), preferred_element_type=F32
    )
    gram[...] = (whole * (1.0 / BOND_DIM)).astype(BF16)


def gram_of(kept, after):
    return pl.pallas_call(
        gram_kernel,
        out_shape=jax.ShapeDtypeStruct((ROWS, ROWS), BF16),
        in_specs=[pl.BlockSpec(memory_space=pl.ANY)] * len(after) + [VMEM],
        out_specs=VMEM,
        compiler_params=pltpu.CompilerParams(vmem_limit_bytes=GRANT),
        cost_estimate=pl.CostEstimate(flops=10**8, bytes_accessed=10**5, transcendentals=0),
    )(*after, kept)


def total(a, b, c, d):
    return summed([a[...], b[...], c[...], d[...]])


def mix(a, b, c, d, mixing, chosen):
    mixed = jnp.dot(mixing[0], a[...], preferred_element_type=F32)
    for i, part in enumerate((b, c, d)):
        mixed = mixed + jnp.dot(mixing[i + 1], part[...], preferred_element_type=F32)
    return mixed * chosen[...]


VMEM = pl.BlockSpec(memory_space=pltpu.VMEM)


def multiply(prepare, operands, order, weights):
    rows = operands[0].shape[0]
    groups = len(order) // RING**2
    shapes = [jax.ShapeDtypeStruct((RING, rows, BLOCK), BF16)] * (RING * groups)
    if prepare is not None:
        shapes = [jax.ShapeDtypeStruct((rows, BLOCK), BF16), *shapes]
    flops = 2 * rows * BLOCK * BLOCK * RING**2 * groups
    return pl.pallas_call(
        functools.partial(multiply_kernel, prepare, len(operands)),
        out_shape=shapes,
        in_specs=[pl.BlockSpec(memory_space=pltpu.SMEM)] + [VMEM] * (len(operands) + 1),
        out_specs=[VMEM] * len(shapes),
        compiler_params=pltpu.CompilerParams(vmem_limit_bytes=GRANT),
        cost_estimate=pl.CostEstimate(
            flops=flops, bytes_accessed=2**20, transcendentals=0
        ),
    )(order, *operands, weights)


def to_cores(theirs, ours):
    arrived = [swap_cores(theirs[d]) for d in SENT]
    return {d: summed([ours[d], got]).astype(BF16) for d, got in zip(SENT, arrived)}


def along_first(mine):
    got = [lax.ppermute(mine[d], BOND, shifts(d, 0)) for d in (2, 1, 3)]
    return summed([mine[0], *got]).astype(BF16)


def along_second(pieces):
    got = [lax.ppermute(pieces[e], BOND, shifts(e, 1)) for e in (2, 1, 3)]
    return summed([pieces[0], *got]).astype(BF16)


def along_z(array):
    return [array] + [lax.ppermute(array, "z", ring_shift(d)) for d in (1, 2, 3)]


def mixing_kernel(z, operator_tensors, mixing):
    def iota(shape, dim):
        return lax.broadcasted_iota(jnp.int32, shape, dim)

    wide, tall = (ROWS, PHYSICAL * MPO_BOND), (MPO_BOND, ROWS)
    first = z[0] * MPO_BOND
    pick = (iota(wide, 1) == first + lax.rem(iota(wide, 0), MPO_BOND)).astype(BF16)
    spread = (iota(tall, 0) == lax.rem(iota(tall, 1), MPO_BOND)).astype(BF16)
    square = (ROWS, ROWS)
    same = lax.div(iota(square, 0), MPO_BOND) == lax.div(iota(square, 1), MPO_BOND)
    for site in range(SITE_COUNT):
        for d in range(RING):
            weights = operator_tensors[site, lax.rem(z[0] + RING - d, RING)]
            narrow = lax.dot_general(
                pick, weights, (((1,), (1,)), ((), ())), preferred_element_type=F32
            ).astype(BF16)
            full = jnp.dot(narrow, spread, preferred_element_type=F32)
            mixing[site, d] = jnp.where(same, full, 0.0).astype(BF16)


def mixing_weights(operator_tensors):
    return pl.pallas_call(
        mixing_kernel,
        out_shape=jax.ShapeDtypeStruct((SITE_COUNT, RING, ROWS, ROWS), BF16),
        in_specs=[pl.BlockSpec(memory_space=pltpu.SMEM), VMEM],
        out_specs=VMEM,
        compiler_params=pltpu.CompilerParams(vmem_limit_bytes=8 * 2**20),
        cost_estimate=pl.CostEstimate(flops=10**9, bytes_accessed=10**6, transcendentals=0),
    )(lax.axis_index("z").astype(jnp.int32)[None], operator_tensors)


def chosen_columns(kept_columns):
    first = lax.axis_index(BOND) * BLOCK * PHYSICAL
    place = kept_columns - first
    here = (place >= 0) & (place < BLOCK * PHYSICAL) & (place % PHYSICAL == lax.axis_index("z"))
    column = place // PHYSICAL
    digits = jnp.arange(16)[None, :, None]
    high = ((column // 16)[:, None] == digits) & here[:, None]
    low = (column % 16)[:, None] == digits
    counts = jnp.einsum(
        "khn,kln->khl", high.astype(BF16), low.astype(BF16), preferred_element_type=F32
    )
    return (counts > 0.5).astype(F32).reshape(SITE_COUNT, 1, BLOCK)


def chip_gram(grams):
    first = lax.axis_index("core") == 0
    got = swap_cores(jnp.where(first, grams[1], grams[0]))
    whole = summed([jnp.where(first, grams[0], grams[1]), got])
    whole = summed(along_z(whole.astype(BF16))).astype(BF16)
    return jnp.pad(whole, ((0, 0), (0, BLOCK - ROWS)))


def both_grams(own):
    other = swap_cores(own)
    first = lax.axis_index("core") == 0
    return jnp.stack([jnp.where(first, own, other), jnp.where(first, other, own)])


def on_device(carried, site_tensors, operator_tensors, rotation, kept_columns):
    core = lax.axis_index("core")
    their_order, our_order = block_order(1 - core), block_order(core)
    tensors = site_tensors.reshape(SITE_COUNT * BLOCK, BOND_DIM)
    turns = rotation.reshape(SITE_COUNT * BLOCK, BOND_DIM)
    mixing = mixing_weights(operator_tensors)
    chosen = chosen_columns(kept_columns)
    grams, near, parts = [], None, None
    for site in range(SITE_COUNT):
        if near is None:
            theirs = multiply_direct(site, carried, their_order, tensors)
            ours = multiply_direct(site, carried, our_order, tensors)
        else:
            weights = load(site, tensors, near)
            state, *theirs = multiply(total, parts, their_order, weights)
            ours = multiply(None, [state], our_order, weights)
        near = along_first(to_cores(theirs, ours))
        parts = along_z(along_second([near[e] for e in range(RING)]))
        weights = load(site, turns, near)
        mixed = [*parts, mixing[site], chosen[site]]
        kept, *theirs = multiply(mix, mixed, their_order, weights)
        ours = multiply(None, [kept], our_order, weights)
        mine = to_cores(theirs, ours)
        grams.append(gram_of(kept, [mine[d] for d in (1, 2, 3)]))
        near = along_first(mine)
        pieces = [near[e] for e in range(RING)]
        if site == SITE_COUNT - 1:
            gram = chip_gram(grams)
            both = along_second([jnp.stack([piece, gram]) for piece in pieces])
            state = summed(along_z(both[0])).astype(BF16)
            got = [lax.ppermute(both[1], BOND, shifts(d, 0)) for d in (1, 2, 3)]
            return state, both_grams(summed([both[1], *got])[:, :ROWS])
        parts = along_z(along_second(pieces))


def solution(mesh):
    finer = Mesh(mesh.devices.reshape(RING, RING, 2, mesh.shape["mpo"]), (*BOND, "z"))
    placed = (P(None, BOND), P(None, BOND, "z", None), P(), P(None, BOND, "z", None), P())
    return jax.shard_map(
        on_device, mesh=finer, in_specs=placed, out_specs=(P(None, BOND), P()), check_vma=False
    )
```

```python
import functools

import jax
import jax.numpy as jnp
from jax import lax
from jax.experimental import pallas as pl
from jax.experimental.pallas import tpu as pltpu
from jax.sharding import Mesh
from jax.sharding import PartitionSpec as P


BOND_DIM = 8192
PHYSICAL = 4
MPO_BOND = 66
LEFT_ROWS = 3
SITE_COUNT = 2
ROWS = LEFT_ROWS * MPO_BOND
BOND = ("y", "x", "core")
RING = 4
BLOCK = 256
SENT = (2, 1, 3, 0)
LOADS = 8
LOAD_GRANT = 48 * 2**20
GRANT = 16 * 2**20
F32 = jnp.float32
BF16 = jnp.bfloat16


def summed(terms):
    total = terms[0].astype(F32)
    for term in terms[1:]:
        total = total + term.astype(F32)
    return total


def chip_device(y, x, core):
    return (y % RING * RING + x % RING) * 2 + core


def shifts(step, x_core):
    pairs = []
    for y in range(RING):
        for x in range(RING):
            pairs.append((chip_device(y, x, x_core), chip_device(y, x + step, x_core)))
            other = 1 - x_core
            pairs.append((chip_device(y, x, other), chip_device(y + step, x, other)))
    return pairs


def ring_shift(step):
    return [(i, (i + step) % RING) for i in range(RING)]


def swap_cores(array):
    return lax.ppermute(array, "core", [(0, 1), (1, 0)])


def block_order(core):
    y, x = lax.axis_index("y"), lax.axis_index("x")
    far = jnp.repeat(jnp.arange(RING), RING)
    near = jnp.tile(jnp.arange(RING), RING)
    dy = jnp.where(core == 0, near, far)
    dx = jnp.where(core == 0, far, near)
    return (((y + dy) % RING * RING + (x + dx) % RING) * 2 + core).astype(jnp.int32)


def load_kernel(site, weights, *rest):
    loaded, sems = rest[-2:]
    rows = BLOCK // LOADS
    copies = []
    for i in range(LOADS):
        source = weights.at[pl.ds(site * BLOCK + i * rows, rows), :]
        copies.append(
            pltpu.make_async_copy(source, loaded.at[pl.ds(i * rows, rows), :], sems.at[i])
        )
        copies[-1].start()
    for copy in copies:
        copy.wait()


def load(site, weights, *after):
    return pl.pallas_call(
        functools.partial(load_kernel, site),
        out_shape=jax.ShapeDtypeStruct((BLOCK, BOND_DIM), BF16),
        in_specs=[pl.BlockSpec(memory_space=pl.ANY)] * (1 + len(after)),
        out_specs=VMEM,
        scratch_shapes=[pltpu.SemaphoreType.DMA((LOADS,))],
        compiler_params=pltpu.CompilerParams(vmem_limit_bytes=LOAD_GRANT),
        cost_estimate=pl.CostEstimate(flops=0, bytes_accessed=4 * 2**20, transcendentals=0),
    )(weights, *after)


def multiply_kernel(prepare, given, order, *refs):
    operands, weights, refs = refs[:given], refs[given], refs[given + 1 :]
    if prepare is None:
        left, outs = operands[0], refs
    else:
        left, outs = refs[0], refs[1:]
        left[...] = prepare(*operands).astype(BF16)
    for group in range(len(outs) // RING):
        for d in SENT:
            for e in range(RING):
                number = order[(group * RING + d) * RING + e]
                columns = weights[:, pl.ds(pl.multiple_of(number * BLOCK, BLOCK), BLOCK)]
                product = jnp.dot(left[...], columns, preferred_element_type=F32)
                outs[group * RING + d][e] = product.astype(BF16)


def gram_kernel(kept, gram):
    whole = lax.dot_general(
        kept[...], kept[...], (((1,), (1,)), ((), ())), preferred_element_type=F32
    )
    gram[...] = (whole * (1.0 / BOND_DIM)).astype(BF16)


def gram_of(kept):
    return pl.pallas_call(
        gram_kernel,
        out_shape=jax.ShapeDtypeStruct((ROWS, ROWS), BF16),
        in_specs=[VMEM],
        out_specs=VMEM,
        compiler_params=pltpu.CompilerParams(vmem_limit_bytes=GRANT),
        cost_estimate=pl.CostEstimate(flops=10**8, bytes_accessed=10**5, transcendentals=0),
    )(kept)


def total(a, b, c, d):
    return summed([a[...], b[...], c[...], d[...]])


def mix(a, b, c, d, mixing, chosen):
    mixed = jnp.dot(mixing[0], a[...], preferred_element_type=F32)
    for i, part in enumerate((b, c, d)):
        mixed = mixed + jnp.dot(mixing[i + 1], part[...], preferred_element_type=F32)
    return mixed * chosen[...]


VMEM = pl.BlockSpec(memory_space=pltpu.VMEM)


def multiply(prepare, operands, order, weights):
    rows = operands[0].shape[0]
    groups = len(order) // RING**2
    shapes = [jax.ShapeDtypeStruct((RING, rows, BLOCK), BF16)] * (RING * groups)
    if prepare is not None:
        shapes = [jax.ShapeDtypeStruct((rows, BLOCK), BF16), *shapes]
    flops = 2 * rows * BLOCK * BLOCK * RING**2 * groups
    return pl.pallas_call(
        functools.partial(multiply_kernel, prepare, len(operands)),
        out_shape=shapes,
        in_specs=[pl.BlockSpec(memory_space=pltpu.SMEM)] + [VMEM] * (len(operands) + 1),
        out_specs=[VMEM] * len(shapes),
        compiler_params=pltpu.CompilerParams(vmem_limit_bytes=GRANT),
        cost_estimate=pl.CostEstimate(
            flops=flops, bytes_accessed=2**20, transcendentals=0
        ),
    )(order, *operands, weights)


def to_cores(theirs, ours):
    arrived = [swap_cores(theirs[d]) for d in SENT]
    return {d: summed([ours[d], got]).astype(BF16) for d, got in zip(SENT, arrived)}


def along_first(mine):
    got = [lax.ppermute(mine[d], BOND, shifts(d, 0)) for d in (2, 1, 3)]
    return summed([mine[0], *got]).astype(BF16)


def along_second(pieces):
    got = [lax.ppermute(pieces[e], BOND, shifts(e, 1)) for e in (2, 1, 3)]
    return summed([pieces[0], *got]).astype(BF16)


def along_z(array):
    return [array] + [lax.ppermute(array, "z", ring_shift(d)) for d in (1, 2, 3)]


def mixing_kernel(z, near, operator_tensors, mixing):
    def iota(shape, dim):
        return lax.broadcasted_iota(jnp.int32, shape, dim)

    wide, tall = (ROWS, PHYSICAL * MPO_BOND), (MPO_BOND, ROWS)
    first = z[0] * MPO_BOND
    pick = (iota(wide, 1) == first + lax.rem(iota(wide, 0), MPO_BOND)).astype(BF16)
    spread = (iota(tall, 0) == lax.rem(iota(tall, 1), MPO_BOND)).astype(BF16)
    square = (ROWS, ROWS)
    same = lax.div(iota(square, 0), MPO_BOND) == lax.div(iota(square, 1), MPO_BOND)
    for site in range(SITE_COUNT):
        for d in range(RING):
            weights = operator_tensors[site, lax.rem(z[0] + RING - d, RING)]
            narrow = lax.dot_general(
                pick, weights, (((1,), (1,)), ((), ())), preferred_element_type=F32
            ).astype(BF16)
            full = jnp.dot(narrow, spread, preferred_element_type=F32)
            mixing[site, d] = jnp.where(same, full, 0.0).astype(BF16)


def mixing_weights(operator_tensors, near):
    return pl.pallas_call(
        mixing_kernel,
        out_shape=jax.ShapeDtypeStruct((SITE_COUNT, RING, ROWS, ROWS), BF16),
        in_specs=[
            pl.BlockSpec(memory_space=pltpu.SMEM),
            pl.BlockSpec(memory_space=pl.ANY),
            VMEM,
        ],
        out_specs=VMEM,
        compiler_params=pltpu.CompilerParams(vmem_limit_bytes=8 * 2**20),
        cost_estimate=pl.CostEstimate(flops=10**9, bytes_accessed=10**6, transcendentals=0),
    )(lax.axis_index("z").astype(jnp.int32)[None], near, operator_tensors)


def chosen_kernel(place, near, kept_columns, chosen):
    def iota(shape, dim):
        return lax.broadcasted_iota(jnp.int32, shape, dim)

    digits, wide = (16, kept_columns.shape[-1]), (16, BLOCK)
    high_of = lax.div(iota(wide, 1), 16) == iota(wide, 0)
    low_of = (lax.rem(iota(wide, 1), 16) == iota(wide, 0)).astype(F32)
    for site in range(SITE_COUNT):
        number = kept_columns[site : site + 1, :] - place[0]
        here = (number >= 0) & (number < BLOCK * PHYSICAL) & (lax.rem(number, PHYSICAL) == place[1])
        column = jnp.where(here, lax.div(number, PHYSICAL), -1)
        high = (lax.div(column, 16) == iota(digits, 0)) & (column >= 0)
        low = lax.rem(column, 16) == iota(digits, 0)
        counts = lax.dot_general(
            high.astype(F32).astype(BF16),
            low.astype(F32).astype(BF16),
            (((1,), (1,)), ((), ())),
            preferred_element_type=F32,
        )
        spread = jnp.dot(counts, low_of, preferred_element_type=F32)
        total = jnp.sum(jnp.where(high_of, spread, 0.0), axis=0, keepdims=True)
        chosen[site] = (total > 0.5).astype(F32)


def chosen_columns(kept_columns, near):
    place = jnp.stack([lax.axis_index(BOND) * BLOCK * PHYSICAL, lax.axis_index("z")])
    return pl.pallas_call(
        chosen_kernel,
        out_shape=jax.ShapeDtypeStruct((SITE_COUNT, 1, BLOCK), F32),
        in_specs=[
            pl.BlockSpec(memory_space=pltpu.SMEM),
            pl.BlockSpec(memory_space=pl.ANY),
            VMEM,
        ],
        out_specs=VMEM,
        compiler_params=pltpu.CompilerParams(vmem_limit_bytes=GRANT),
        cost_estimate=pl.CostEstimate(flops=10**8, bytes_accessed=10**5, transcendentals=0),
    )(place.astype(jnp.int32), near, kept_columns)


def chip_gram(grams):
    first = lax.axis_index("core") == 0
    got = swap_cores(jnp.where(first, grams[1], grams[0]))
    whole = summed([jnp.where(first, grams[0], grams[1]), got])
    whole = summed(along_z(whole.astype(BF16))).astype(BF16)
    return jnp.pad(whole, ((0, 0), (0, BLOCK - ROWS)))


def finish_kernel(core, a, b, c, d, own, other, state, grams):
    state[...] = total(a, b, c, d).astype(BF16)
    grams[core[0]] = own[...]
    grams[1 - core[0]] = other[...]


def finish(parts, own):
    return pl.pallas_call(
        finish_kernel,
        out_shape=[
            jax.ShapeDtypeStruct((ROWS, BLOCK), BF16),
            jax.ShapeDtypeStruct((SITE_COUNT, ROWS, ROWS), F32),
        ],
        in_specs=[pl.BlockSpec(memory_space=pltpu.SMEM)] + [VMEM] * 6,
        out_specs=[VMEM] * 2,
        compiler_params=pltpu.CompilerParams(vmem_limit_bytes=GRANT),
    )(lax.axis_index("core").astype(jnp.int32)[None], *parts, own, swap_cores(own))


def on_device(carried, site_tensors, operator_tensors, rotation, kept_columns):
    core = lax.axis_index("core")
    their_order, our_order = block_order(1 - core), block_order(core)
    tensors = site_tensors.reshape(SITE_COUNT * BLOCK, BOND_DIM)
    turns = rotation.reshape(SITE_COUNT * BLOCK, BOND_DIM)
    grams, near, parts = [], None, None
    for site in range(SITE_COUNT):
        if near is None:
            both_orders = jnp.concatenate([their_order, our_order])
            pieces = multiply(None, [carried], both_orders, load(site, tensors))
            theirs, ours = pieces[:RING], pieces[RING:]
        else:
            weights = load(site, tensors, near)
            state, *theirs = multiply(total, parts, their_order, weights)
            ours = multiply(None, [state], our_order, weights)
        near = along_first(to_cores(theirs, ours))
        if site == 0:
            mixing = mixing_weights(operator_tensors, near)
            chosen = chosen_columns(kept_columns, near)
        parts = along_z(along_second([near[e] for e in range(RING)]))
        weights = load(site, turns, near)
        mixed = [*parts, mixing[site], chosen[site]]
        kept, *theirs = multiply(mix, mixed, their_order, weights)
        grams.append(gram_of(kept))
        ours = multiply(None, [kept], our_order, weights)
        mine = to_cores(theirs, ours)
        near = along_first(mine)
        pieces = [near[e] for e in range(RING)]
        if site == SITE_COUNT - 1:
            gram = chip_gram(grams)
            both = along_second([jnp.stack([piece, gram]) for piece in pieces])
            parts = along_z(both[0])
            got = [lax.ppermute(both[1], BOND, shifts(d, 0)) for d in (1, 2, 3)]
            return tuple(finish(parts, summed([both[1], *got])[:, :ROWS]))
        parts = along_z(along_second(pieces))


def solution(mesh):
    finer = Mesh(mesh.devices.reshape(RING, RING, 2, mesh.shape["mpo"]), (*BOND, "z"))
    placed = (P(None, BOND), P(None, BOND, "z", None), P(), P(None, BOND, "z", None), P())
    return jax.shard_map(
        on_device, mesh=finer, in_specs=placed, out_specs=(P(None, BOND), P()), check_vma=False
    )
```

```python
import functools

import jax
import jax.numpy as jnp
from jax import lax
from jax.experimental import pallas as pl
from jax.experimental.pallas import tpu as pltpu
from jax.sharding import Mesh
from jax.sharding import PartitionSpec as P


BOND_DIM = 8192
PHYSICAL = 4
MPO_BOND = 66
LEFT_ROWS = 3
SITE_COUNT = 2
ROWS = LEFT_ROWS * MPO_BOND
BOND = ("y", "x", "core")
RING = 4
BLOCK = 256
SENT = (2, 1, 3, 0)
LOADS = 8
LOAD_GRANT = 48 * 2**20
GRANT = 16 * 2**20
F32 = jnp.float32
BF16 = jnp.bfloat16


def summed(terms):
    total = terms[0].astype(F32)
    for term in terms[1:]:
        total = total + term.astype(F32)
    return total


def chip_device(y, x, core):
    return (y % RING * RING + x % RING) * 2 + core


def shifts(step, x_core):
    pairs = []
    for y in range(RING):
        for x in range(RING):
            pairs.append((chip_device(y, x, x_core), chip_device(y, x + step, x_core)))
            other = 1 - x_core
            pairs.append((chip_device(y, x, other), chip_device(y + step, x, other)))
    return pairs


def ring_shift(step):
    return [(i, (i + step) % RING) for i in range(RING)]


def swap_cores(array):
    return lax.ppermute(array, "core", [(0, 1), (1, 0)])


def block_order(core):
    y, x = lax.axis_index("y"), lax.axis_index("x")
    far = jnp.repeat(jnp.arange(RING), RING)
    near = jnp.tile(jnp.arange(RING), RING)
    dy = jnp.where(core == 0, near, far)
    dx = jnp.where(core == 0, far, near)
    return (((y + dy) % RING * RING + (x + dx) % RING) * 2 + core).astype(jnp.int32)


def load_kernel(site, weights, *rest):
    loaded, sems = rest[-2:]
    rows = BLOCK // LOADS
    copies = []
    for i in range(LOADS):
        source = weights.at[pl.ds(site * BLOCK + i * rows, rows), :]
        copies.append(
            pltpu.make_async_copy(source, loaded.at[pl.ds(i * rows, rows), :], sems.at[i])
        )
        copies[-1].start()
    for copy in copies:
        copy.wait()


def load(site, weights, *after):
    return pl.pallas_call(
        functools.partial(load_kernel, site),
        out_shape=jax.ShapeDtypeStruct((BLOCK, BOND_DIM), BF16),
        in_specs=[pl.BlockSpec(memory_space=pl.ANY)] * (1 + len(after)),
        out_specs=VMEM,
        scratch_shapes=[pltpu.SemaphoreType.DMA((LOADS,))],
        compiler_params=pltpu.CompilerParams(vmem_limit_bytes=LOAD_GRANT),
        cost_estimate=pl.CostEstimate(flops=0, bytes_accessed=4 * 2**20, transcendentals=0),
    )(weights, *after)


def multiply_kernel(prepare, given, order, *refs):
    operands, weights, refs = refs[:given], refs[given], refs[given + 1 :]
    if prepare is None:
        left, outs = operands[0], refs
    else:
        left, outs = refs[0], refs[1:]
        left[...] = prepare(*operands).astype(BF16)
    for group in range(len(outs) // RING):
        for d in SENT:
            for e in range(RING):
                number = order[(group * RING + d) * RING + e]
                columns = weights[:, pl.ds(pl.multiple_of(number * BLOCK, BLOCK), BLOCK)]
                product = jnp.dot(left[...], columns, preferred_element_type=F32)
                outs[group * RING + d][e] = product.astype(BF16)


def gram_kernel(kept, gram):
    whole = lax.dot_general(
        kept[...], kept[...], (((1,), (1,)), ((), ())), preferred_element_type=F32
    )
    gram[...] = (whole * (1.0 / BOND_DIM)).astype(BF16)


def gram_of(kept):
    return pl.pallas_call(
        gram_kernel,
        out_shape=jax.ShapeDtypeStruct((ROWS, ROWS), BF16),
        in_specs=[VMEM],
        out_specs=VMEM,
        compiler_params=pltpu.CompilerParams(vmem_limit_bytes=GRANT),
        cost_estimate=pl.CostEstimate(flops=10**8, bytes_accessed=10**5, transcendentals=0),
    )(kept)


def total(a, b, c, d):
    return summed([a[...], b[...], c[...], d[...]])


def mix(a, b, c, d, mixing, chosen):
    mixed = jnp.dot(mixing[0], a[...], preferred_element_type=F32)
    for i, part in enumerate((b, c, d)):
        mixed = mixed + jnp.dot(mixing[i + 1], part[...], preferred_element_type=F32)
    return mixed * chosen[...]


VMEM = pl.BlockSpec(memory_space=pltpu.VMEM)


def multiply(prepare, operands, order, weights):
    rows = operands[0].shape[0]
    groups = len(order) // RING**2
    shapes = [jax.ShapeDtypeStruct((RING, rows, BLOCK), BF16)] * (RING * groups)
    if prepare is not None:
        shapes = [jax.ShapeDtypeStruct((rows, BLOCK), BF16), *shapes]
    flops = 2 * rows * BLOCK * BLOCK * RING**2 * groups
    return pl.pallas_call(
        functools.partial(multiply_kernel, prepare, len(operands)),
        out_shape=shapes,
        in_specs=[pl.BlockSpec(memory_space=pltpu.SMEM)] + [VMEM] * (len(operands) + 1),
        out_specs=[VMEM] * len(shapes),
        compiler_params=pltpu.CompilerParams(vmem_limit_bytes=GRANT),
        cost_estimate=pl.CostEstimate(
            flops=flops, bytes_accessed=2**20, transcendentals=0
        ),
    )(order, *operands, weights)


def to_cores(theirs, ours):
    arrived = [swap_cores(theirs[d]) for d in SENT]
    return {d: summed([ours[d], got]).astype(BF16) for d, got in zip(SENT, arrived)}


def along_first(mine):
    got = [lax.ppermute(mine[d], BOND, shifts(d, 0)) for d in (2, 1, 3)]
    return summed([mine[0], *got]).astype(BF16)


def along_second(pieces):
    got = [lax.ppermute(pieces[e], BOND, shifts(e, 1)) for e in (2, 1, 3)]
    return summed([pieces[0], *got]).astype(BF16)


def along_z(array):
    return [array] + [lax.ppermute(array, "z", ring_shift(d)) for d in (1, 2, 3)]


def mixing_kernel(z, near, operator_tensors, mixing):
    def iota(shape, dim):
        return lax.broadcasted_iota(jnp.int32, shape, dim)

    wide, tall = (ROWS, PHYSICAL * MPO_BOND), (MPO_BOND, ROWS)
    first = z[0] * MPO_BOND
    pick = (iota(wide, 1) == first + lax.rem(iota(wide, 0), MPO_BOND)).astype(BF16)
    spread = (iota(tall, 0) == lax.rem(iota(tall, 1), MPO_BOND)).astype(BF16)
    square = (ROWS, ROWS)
    same = lax.div(iota(square, 0), MPO_BOND) == lax.div(iota(square, 1), MPO_BOND)
    for site in range(SITE_COUNT):
        for d in range(RING):
            weights = operator_tensors[site, lax.rem(z[0] + RING - d, RING)]
            narrow = lax.dot_general(
                pick, weights, (((1,), (1,)), ((), ())), preferred_element_type=F32
            ).astype(BF16)
            full = jnp.dot(narrow, spread, preferred_element_type=F32)
            mixing[site, d] = jnp.where(same, full, 0.0).astype(BF16)


def mixing_weights(operator_tensors, near):
    return pl.pallas_call(
        mixing_kernel,
        out_shape=jax.ShapeDtypeStruct((SITE_COUNT, RING, ROWS, ROWS), BF16),
        in_specs=[
            pl.BlockSpec(memory_space=pltpu.SMEM),
            pl.BlockSpec(memory_space=pl.ANY),
            VMEM,
        ],
        out_specs=VMEM,
        compiler_params=pltpu.CompilerParams(vmem_limit_bytes=8 * 2**20),
        cost_estimate=pl.CostEstimate(flops=10**9, bytes_accessed=10**6, transcendentals=0),
    )(lax.axis_index("z").astype(jnp.int32)[None], near, operator_tensors)


def chosen_kernel(place, near, kept_columns, chosen):
    def iota(shape, dim):
        return lax.broadcasted_iota(jnp.int32, shape, dim)

    digits, wide = (16, kept_columns.shape[-1]), (16, BLOCK)
    high_of = lax.div(iota(wide, 1), 16) == iota(wide, 0)
    low_of = (lax.rem(iota(wide, 1), 16) == iota(wide, 0)).astype(F32)
    for site in range(SITE_COUNT):
        number = kept_columns[site : site + 1, :] - place[0]
        here = (number >= 0) & (number < BLOCK * PHYSICAL) & (lax.rem(number, PHYSICAL) == place[1])
        column = jnp.where(here, lax.div(number, PHYSICAL), -1)
        high = (lax.div(column, 16) == iota(digits, 0)) & (column >= 0)
        low = lax.rem(column, 16) == iota(digits, 0)
        counts = lax.dot_general(
            high.astype(F32).astype(BF16),
            low.astype(F32).astype(BF16),
            (((1,), (1,)), ((), ())),
            preferred_element_type=F32,
        )
        spread = jnp.dot(counts, low_of, preferred_element_type=F32)
        total = jnp.sum(jnp.where(high_of, spread, 0.0), axis=0, keepdims=True)
        chosen[site] = (total > 0.5).astype(F32)


def chosen_columns(kept_columns, near):
    place = jnp.stack([lax.axis_index(BOND) * BLOCK * PHYSICAL, lax.axis_index("z")])
    return pl.pallas_call(
        chosen_kernel,
        out_shape=jax.ShapeDtypeStruct((SITE_COUNT, 1, BLOCK), F32),
        in_specs=[
            pl.BlockSpec(memory_space=pltpu.SMEM),
            pl.BlockSpec(memory_space=pl.ANY),
            VMEM,
        ],
        out_specs=VMEM,
        compiler_params=pltpu.CompilerParams(vmem_limit_bytes=GRANT),
        cost_estimate=pl.CostEstimate(flops=10**8, bytes_accessed=10**5, transcendentals=0),
    )(place.astype(jnp.int32), near, kept_columns)


def chip_gram(grams):
    first = lax.axis_index("core") == 0
    got = swap_cores(jnp.where(first, grams[1], grams[0]))
    whole = summed([jnp.where(first, grams[0], grams[1]), got])
    whole = summed(along_z(whole.astype(BF16))).astype(BF16)
    return jnp.pad(whole, ((0, 0), (0, BLOCK - ROWS)))


def finish_kernel(core, own, other, grams):
    mine, theirs = own[...], other[...]
    first = core[0] == 0
    grams[:, 0, :] = jnp.where(first, mine, theirs)
    grams[:, 1, :] = jnp.where(first, theirs, mine)


def both_grams(own):
    grams = pl.pallas_call(
        finish_kernel,
        out_shape=jax.ShapeDtypeStruct((ROWS, SITE_COUNT, ROWS), F32),
        in_specs=[pl.BlockSpec(memory_space=pltpu.SMEM)] + [VMEM] * 2,
        out_specs=VMEM,
        compiler_params=pltpu.CompilerParams(vmem_limit_bytes=GRANT),
    )(lax.axis_index("core").astype(jnp.int32)[None], own, swap_cores(own))
    return jnp.swapaxes(grams, 0, 1)


def on_device(carried, site_tensors, operator_tensors, rotation, kept_columns):
    core = lax.axis_index("core")
    their_order, our_order = block_order(1 - core), block_order(core)
    tensors = site_tensors.reshape(SITE_COUNT * BLOCK, BOND_DIM)
    turns = rotation.reshape(SITE_COUNT * BLOCK, BOND_DIM)
    grams, near, parts = [], None, None
    for site in range(SITE_COUNT):
        if near is None:
            both_orders = jnp.concatenate([their_order, our_order])
            pieces = multiply(None, [carried], both_orders, load(site, tensors))
            theirs, ours = pieces[:RING], pieces[RING:]
        else:
            weights = load(site, tensors, near)
            state, *theirs = multiply(total, parts, their_order, weights)
            ours = multiply(None, [state], our_order, weights)
        mine = to_cores(theirs, ours)
        near = along_first(mine)
        if site == 0:
            mixing = mixing_weights(operator_tensors, mine[SENT[2]])
            chosen = chosen_columns(kept_columns, near)
        parts = along_z(along_second([near[e] for e in range(RING)]))
        weights = load(site, turns, near)
        mixed = [*parts, mixing[site], chosen[site]]
        kept, *theirs = multiply(mix, mixed, their_order, weights)
        grams.append(gram_of(kept))
        ours = multiply(None, [kept], our_order, weights)
        mine = to_cores(theirs, ours)
        near = along_first(mine)
        pieces = [near[e] for e in range(RING)]
        if site == SITE_COUNT - 1:
            gram = chip_gram(grams)
            both = along_second([jnp.stack([piece, gram]) for piece in pieces])
            parts, got = [both[0]], []
            for d in (2, 1, 3):
                got.append(lax.ppermute(both[1], BOND, shifts(d, 0)))
            for d in (2, 1, 3):
                parts.append(lax.ppermute(both[0], "z", ring_shift(d)))
            grams = both_grams(summed([both[1], *got])[:, :ROWS])
            return summed(parts).astype(BF16), grams
        parts = along_z(along_second(pieces))


def solution(mesh):
    finer = Mesh(mesh.devices.reshape(RING, RING, 2, mesh.shape["mpo"]), (*BOND, "z"))
    placed = (P(None, BOND), P(None, BOND, "z", None), P(), P(None, BOND, "z", None), P())
    return jax.shard_map(
        on_device, mesh=finer, in_specs=placed, out_specs=(P(None, BOND), P()), check_vma=False
    )
```

```python
import functools

import jax
import jax.numpy as jnp
from jax import lax
from jax.experimental import pallas as pl
from jax.experimental.pallas import tpu as pltpu
from jax.sharding import Mesh
from jax.sharding import PartitionSpec as P


BOND_DIM = 8192
PHYSICAL = 4
MPO_BOND = 66
LEFT_ROWS = 3
SITE_COUNT = 2
ROWS = LEFT_ROWS * MPO_BOND
BOND = ("y", "x", "core")
RING = 4
BLOCK = 256
PLACE = 2 * RING**2
SENT = (2, 1, 3, 0)
LOADS = 8
LOAD_GRANT = 48 * 2**20
GRANT = 16 * 2**20
F32 = jnp.float32
BF16 = jnp.bfloat16


def summed(terms):
    total = terms[0].astype(F32)
    for term in terms[1:]:
        total = total + term.astype(F32)
    return total


def chip_device(y, x, core):
    return (y % RING * RING + x % RING) * 2 + core


def shifts(step, x_core):
    pairs = []
    for y in range(RING):
        for x in range(RING):
            pairs.append((chip_device(y, x, x_core), chip_device(y, x + step, x_core)))
            other = 1 - x_core
            pairs.append((chip_device(y, x, other), chip_device(y + step, x, other)))
    return pairs


def ring_shift(step):
    return [(i, (i + step) % RING) for i in range(RING)]


def swap_cores(array):
    return lax.ppermute(array, "core", [(0, 1), (1, 0)])


def block_order(core):
    y, x = lax.axis_index("y"), lax.axis_index("x")
    far = jnp.repeat(jnp.arange(RING), RING)
    near = jnp.tile(jnp.arange(RING), RING)
    dy = jnp.where(core == 0, near, far)
    dx = jnp.where(core == 0, far, near)
    return (((y + dy) % RING * RING + (x + dx) % RING) * 2 + core).astype(jnp.int32)


def load_kernel(site, weights, *rest):
    loaded, sems = rest[-2:]
    rows = BLOCK // LOADS
    copies = []
    for i in range(LOADS):
        source = weights.at[pl.ds(site * BLOCK + i * rows, rows), :]
        copies.append(
            pltpu.make_async_copy(source, loaded.at[pl.ds(i * rows, rows), :], sems.at[i])
        )
        copies[-1].start()
    for copy in copies:
        copy.wait()


def load(site, weights, *after):
    return pl.pallas_call(
        functools.partial(load_kernel, site),
        out_shape=jax.ShapeDtypeStruct((BLOCK, BOND_DIM), BF16),
        in_specs=[pl.BlockSpec(memory_space=pl.ANY)] * (1 + len(after)),
        out_specs=VMEM,
        scratch_shapes=[pltpu.SemaphoreType.DMA((LOADS,))],
        compiler_params=pltpu.CompilerParams(vmem_limit_bytes=LOAD_GRANT),
        cost_estimate=pl.CostEstimate(flops=0, bytes_accessed=4 * 2**20, transcendentals=0),
    )(weights, *after)


def multiply_kernel(prepare, given, order, *refs):
    operands, weights, refs = refs[:given], refs[given], refs[given + 1 :]
    if prepare is None:
        left, outs = operands[0], refs
    else:
        left, outs = refs[0], refs[1:]
        left[...] = prepare(*operands).astype(BF16)
    for group in range(len(outs) // RING):
        for d in SENT:
            for e in range(RING):
                number = order[(group * RING + d) * RING + e]
                columns = weights[:, pl.ds(pl.multiple_of(number * BLOCK, BLOCK), BLOCK)]
                product = jnp.dot(left[...], columns, preferred_element_type=F32)
                outs[group * RING + d][e] = product.astype(BF16)


def gram_kernel(kept, gram):
    whole = lax.dot_general(
        kept[...], kept[...], (((1,), (1,)), ((), ())), preferred_element_type=F32
    )
    gram[...] = (whole * (1.0 / BOND_DIM)).astype(BF16)


def gram_of(kept):
    return pl.pallas_call(
        gram_kernel,
        out_shape=jax.ShapeDtypeStruct((ROWS, ROWS), BF16),
        in_specs=[VMEM],
        out_specs=VMEM,
        compiler_params=pltpu.CompilerParams(vmem_limit_bytes=GRANT),
        cost_estimate=pl.CostEstimate(flops=10**8, bytes_accessed=10**5, transcendentals=0),
    )(kept)


def total(a, b, c, d):
    return summed([a[...], b[...], c[...], d[...]])


def mix(a, b, c, d, mixing, chosen):
    mixed = jnp.dot(mixing[0], a[...], preferred_element_type=F32)
    for i, part in enumerate((b, c, d)):
        mixed = mixed + jnp.dot(mixing[i + 1], part[...], preferred_element_type=F32)
    return mixed * chosen[...]


VMEM = pl.BlockSpec(memory_space=pltpu.VMEM)


def multiply(prepare, operands, order, weights):
    rows = operands[0].shape[0]
    groups = len(order) // RING**2
    shapes = [jax.ShapeDtypeStruct((RING, rows, BLOCK), BF16)] * (RING * groups)
    if prepare is not None:
        shapes = [jax.ShapeDtypeStruct((rows, BLOCK), BF16), *shapes]
    flops = 2 * rows * BLOCK * BLOCK * RING**2 * groups
    return pl.pallas_call(
        functools.partial(multiply_kernel, prepare, len(operands)),
        out_shape=shapes,
        in_specs=[pl.BlockSpec(memory_space=pltpu.SMEM)] + [VMEM] * (len(operands) + 1),
        out_specs=[VMEM] * len(shapes),
        compiler_params=pltpu.CompilerParams(vmem_limit_bytes=GRANT),
        cost_estimate=pl.CostEstimate(
            flops=flops, bytes_accessed=2**20, transcendentals=0
        ),
    )(order, *operands, weights)


def to_cores(theirs, ours):
    arrived = [swap_cores(theirs[d]) for d in SENT]
    return {d: summed([ours[d], got]).astype(BF16) for d, got in zip(SENT, arrived)}


def along_first(mine):
    got = [lax.ppermute(mine[d], BOND, shifts(d, 0)) for d in (2, 1, 3)]
    return summed([mine[0], *got]).astype(BF16)


def along_second(pieces):
    got = [lax.ppermute(pieces[e], BOND, shifts(e, 1)) for e in (2, 1, 3)]
    return summed([pieces[0], *got]).astype(BF16)


def along_z(array):
    return [array] + [lax.ppermute(array, "z", ring_shift(d)) for d in (1, 2, 3)]


def mixing_kernel(place, near, operator_tensors, mixing):
    def iota(shape, dim):
        return lax.broadcasted_iota(jnp.int32, shape, dim)

    wide, tall = (ROWS, PHYSICAL * MPO_BOND), (MPO_BOND, ROWS)
    first = place[PLACE + 1] * MPO_BOND
    pick = (iota(wide, 1) == first + lax.rem(iota(wide, 0), MPO_BOND)).astype(BF16)
    spread = (iota(tall, 0) == lax.rem(iota(tall, 1), MPO_BOND)).astype(BF16)
    square = (ROWS, ROWS)
    same = lax.div(iota(square, 0), MPO_BOND) == lax.div(iota(square, 1), MPO_BOND)
    for site in range(SITE_COUNT):
        whole = operator_tensors[site].astype(F32)
        planes = [whole[:, number, :] for number in range(PHYSICAL)]
        for d in range(RING):
            turned = lax.rem(place[PLACE + 1] + RING - d, RING)
            weights = planes[0]
            for number in range(1, PHYSICAL):
                weights = jnp.where(turned == number, planes[number], weights)
            weights = weights.astype(BF16)
            narrow = lax.dot_general(
                pick, weights, (((1,), (1,)), ((), ())), preferred_element_type=F32
            ).astype(BF16)
            full = jnp.dot(narrow, spread, preferred_element_type=F32)
            mixing[site, d] = jnp.where(same, full, 0.0).astype(BF16)


def mixing_weights(operator_tensors, place, near):
    return pl.pallas_call(
        mixing_kernel,
        out_shape=jax.ShapeDtypeStruct((SITE_COUNT, RING, ROWS, ROWS), BF16),
        in_specs=[
            pl.BlockSpec(memory_space=pltpu.SMEM),
            pl.BlockSpec(memory_space=pl.ANY),
            VMEM,
        ],
        out_specs=VMEM,
        compiler_params=pltpu.CompilerParams(vmem_limit_bytes=8 * 2**20),
        cost_estimate=pl.CostEstimate(flops=10**9, bytes_accessed=10**6, transcendentals=0),
    )(place, near, jnp.swapaxes(operator_tensors, 1, 2))


def chosen_kernel(place, near, kept_columns, chosen):
    def iota(shape, dim):
        return lax.broadcasted_iota(jnp.int32, shape, dim)

    digits, wide = (16, kept_columns.shape[-1]), (16, BLOCK)
    high_of = lax.div(iota(wide, 1), 16) == iota(wide, 0)
    low_of = (lax.rem(iota(wide, 1), 16) == iota(wide, 0)).astype(F32)
    for site in range(SITE_COUNT):
        number = kept_columns[site : site + 1, :] - place[PLACE]
        here = (number >= 0) & (number < BLOCK * PHYSICAL) & (lax.rem(number, PHYSICAL) == place[PLACE + 1])
        column = jnp.where(here, lax.div(number, PHYSICAL), -1)
        high = (lax.div(column, 16) == iota(digits, 0)) & (column >= 0)
        low = lax.rem(column, 16) == iota(digits, 0)
        counts = lax.dot_general(
            high.astype(F32).astype(BF16),
            low.astype(F32).astype(BF16),
            (((1,), (1,)), ((), ())),
            preferred_element_type=F32,
        )
        spread = jnp.dot(counts, low_of, preferred_element_type=F32)
        total = jnp.sum(jnp.where(high_of, spread, 0.0), axis=0, keepdims=True)
        chosen[site] = (total > 0.5).astype(F32)


def chosen_columns(kept_columns, place, near):
    return pl.pallas_call(
        chosen_kernel,
        out_shape=jax.ShapeDtypeStruct((SITE_COUNT, 1, BLOCK), F32),
        in_specs=[
            pl.BlockSpec(memory_space=pltpu.SMEM),
            pl.BlockSpec(memory_space=pl.ANY),
            VMEM,
        ],
        out_specs=VMEM,
        compiler_params=pltpu.CompilerParams(vmem_limit_bytes=GRANT),
        cost_estimate=pl.CostEstimate(flops=10**8, bytes_accessed=10**5, transcendentals=0),
    )(place, near, kept_columns)


def chip_gram(grams):
    first = lax.axis_index("core") == 0
    got = swap_cores(jnp.where(first, grams[1], grams[0]))
    whole = summed([jnp.where(first, grams[0], grams[1]), got])
    whole = summed(along_z(whole.astype(BF16))).astype(BF16)
    return jnp.pad(whole, ((0, 0), (0, BLOCK - ROWS)))


def finish_kernel(core, own, other, grams):
    mine, theirs = own[...], other[...]
    first = core[0] == 0
    grams[:, 0, :] = jnp.where(first, mine, theirs)
    grams[:, 1, :] = jnp.where(first, theirs, mine)


def both_grams(own):
    grams = pl.pallas_call(
        finish_kernel,
        out_shape=jax.ShapeDtypeStruct((ROWS, SITE_COUNT, ROWS), F32),
        in_specs=[pl.BlockSpec(memory_space=pltpu.SMEM)] + [VMEM] * 2,
        out_specs=VMEM,
        compiler_params=pltpu.CompilerParams(vmem_limit_bytes=GRANT),
    )(lax.axis_index("core").astype(jnp.int32)[None], own, swap_cores(own))
    return jnp.swapaxes(grams, 0, 1)


def on_device(carried, site_tensors, operator_tensors, rotation, kept_columns):
    core = lax.axis_index("core")
    their_order, our_order = block_order(1 - core), block_order(core)
    own = jnp.stack([lax.axis_index(BOND) * BLOCK * PHYSICAL, lax.axis_index("z")])
    places = jnp.concatenate([their_order, our_order, own.astype(jnp.int32)])
    tensors = site_tensors.reshape(SITE_COUNT * BLOCK, BOND_DIM)
    turns = rotation.reshape(SITE_COUNT * BLOCK, BOND_DIM)
    grams, near, parts = [], None, None
    for site in range(SITE_COUNT):
        if near is None:
            pieces = multiply(None, [carried], places, load(site, tensors, places))
            theirs, ours = pieces[:RING], pieces[RING:]
        else:
            weights = load(site, tensors, near)
            state, *theirs = multiply(total, parts, their_order, weights)
            ours = multiply(None, [state], our_order, weights)
        mine = to_cores(theirs, ours)
        near = along_first(mine)
        if site == 0:
            mixing = mixing_weights(operator_tensors, places, mine[SENT[2]])
            chosen = chosen_columns(kept_columns, places, near)
        parts = along_z(along_second([near[e] for e in range(RING)]))
        weights = load(site, turns, near)
        mixed = [*parts, mixing[site], chosen[site]]
        kept, *theirs = multiply(mix, mixed, their_order, weights)
        grams.append(gram_of(kept))
        ours = multiply(None, [kept], our_order, weights)
        mine = to_cores(theirs, ours)
        near = along_first(mine)
        pieces = [near[e] for e in range(RING)]
        if site == SITE_COUNT - 1:
            gram = chip_gram(grams)
            both = along_second([jnp.stack([piece, gram]) for piece in pieces])
            parts, got = [both[0]], []
            for d in (2, 1, 3):
                got.append(lax.ppermute(both[1], BOND, shifts(d, 0)))
            for d in (2, 1, 3):
                parts.append(lax.ppermute(both[0], "z", ring_shift(d)))
            grams = both_grams(summed([both[1], *got])[:, :ROWS])
            return summed(parts).astype(BF16), grams
        parts = along_z(along_second(pieces))


def solution(mesh):
    finer = Mesh(mesh.devices.reshape(RING, RING, 2, mesh.shape["mpo"]), (*BOND, "z"))
    placed = (P(None, BOND), P(None, BOND, "z", None), P(), P(None, BOND, "z", None), P())
    return jax.shard_map(
        on_device, mesh=finer, in_specs=placed, out_specs=(P(None, BOND), P()), check_vma=False
    )
```

```python
import functools

import jax
import jax.numpy as jnp
from jax import lax
from jax.experimental import pallas as pl
from jax.experimental.pallas import tpu as pltpu
from jax.sharding import Mesh
from jax.sharding import PartitionSpec as P


BOND_DIM = 8192
PHYSICAL = 4
MPO_BOND = 66
LEFT_ROWS = 3
SITE_COUNT = 2
ROWS = LEFT_ROWS * MPO_BOND
BOND = ("y", "x", "core")
RING = 4
BLOCK = 256
PLACE = 2 * RING**2
SENT = (2, 1, 3, 0)
LOADS = 8
LOAD_GRANT = 48 * 2**20
GRANT = 16 * 2**20
F32 = jnp.float32
BF16 = jnp.bfloat16


def summed(terms):
    total = terms[0].astype(F32)
    for term in terms[1:]:
        total = total + term.astype(F32)
    return total


def chip_device(y, x, core):
    return (y % RING * RING + x % RING) * 2 + core


def shifts(step, x_core):
    pairs = []
    for y in range(RING):
        for x in range(RING):
            pairs.append((chip_device(y, x, x_core), chip_device(y, x + step, x_core)))
            other = 1 - x_core
            pairs.append((chip_device(y, x, other), chip_device(y + step, x, other)))
    return pairs


def ring_shift(step):
    return [(i, (i + step) % RING) for i in range(RING)]


def swap_cores(array):
    return lax.ppermute(array, "core", [(0, 1), (1, 0)])


def block_order(core):
    y, x = lax.axis_index("y"), lax.axis_index("x")
    far = jnp.repeat(jnp.arange(RING), RING)
    near = jnp.tile(jnp.arange(RING), RING)
    dy = jnp.where(core == 0, near, far)
    dx = jnp.where(core == 0, far, near)
    return (((y + dy) % RING * RING + (x + dx) % RING) * 2 + core).astype(jnp.int32)


def load_kernel(site, weights, *rest):
    loaded, sems = rest[-2:]
    rows = BLOCK // LOADS
    copies = []
    for i in range(LOADS):
        source = weights.at[pl.ds(site * BLOCK + i * rows, rows), :]
        copies.append(
            pltpu.make_async_copy(source, loaded.at[pl.ds(i * rows, rows), :], sems.at[i])
        )
        copies[-1].start()
    for copy in copies:
        copy.wait()


def load(site, weights, *after):
    return pl.pallas_call(
        functools.partial(load_kernel, site),
        out_shape=jax.ShapeDtypeStruct((BLOCK, BOND_DIM), BF16),
        in_specs=[pl.BlockSpec(memory_space=pl.ANY)] * (1 + len(after)),
        out_specs=VMEM,
        scratch_shapes=[pltpu.SemaphoreType.DMA((LOADS,))],
        compiler_params=pltpu.CompilerParams(vmem_limit_bytes=LOAD_GRANT),
        cost_estimate=pl.CostEstimate(flops=0, bytes_accessed=4 * 2**20, transcendentals=0),
    )(weights, *after)


def multiply_kernel(prepare, given, order, *refs):
    operands, weights, refs = refs[:given], refs[given], refs[given + 1 :]
    if prepare is None:
        left, outs = operands[0], refs
    else:
        left, outs = refs[0], refs[1:]
        left[...] = prepare(*operands).astype(BF16)
    for group in range(len(outs) // RING):
        for d in SENT:
            for e in range(RING):
                number = order[(group * RING + d) * RING + e]
                columns = weights[:, pl.ds(pl.multiple_of(number * BLOCK, BLOCK), BLOCK)]
                product = jnp.dot(left[...], columns, preferred_element_type=F32)
                outs[group * RING + d][e] = product.astype(BF16)


def gram_kernel(kept, gram):
    whole = lax.dot_general(
        kept[...], kept[...], (((1,), (1,)), ((), ())), preferred_element_type=F32
    )
    gram[...] = (whole * (1.0 / BOND_DIM)).astype(BF16)


def gram_of(kept):
    return pl.pallas_call(
        gram_kernel,
        out_shape=jax.ShapeDtypeStruct((ROWS, ROWS), BF16),
        in_specs=[VMEM],
        out_specs=VMEM,
        compiler_params=pltpu.CompilerParams(vmem_limit_bytes=GRANT),
        cost_estimate=pl.CostEstimate(flops=10**8, bytes_accessed=10**5, transcendentals=0),
    )(kept)


def total(a, b, c, d):
    return summed([a[...], b[...], c[...], d[...]])


def mix(a, b, c, d, mixing, chosen):
    mixed = jnp.dot(mixing[0], a[...], preferred_element_type=F32)
    for i, part in enumerate((b, c, d)):
        mixed = mixed + jnp.dot(mixing[i + 1], part[...], preferred_element_type=F32)
    return mixed * chosen[...]


VMEM = pl.BlockSpec(memory_space=pltpu.VMEM)


def multiply(prepare, operands, order, weights):
    rows = operands[0].shape[0]
    groups = len(order) // RING**2
    shapes = [jax.ShapeDtypeStruct((RING, rows, BLOCK), BF16)] * (RING * groups)
    if prepare is not None:
        shapes = [jax.ShapeDtypeStruct((rows, BLOCK), BF16), *shapes]
    flops = 2 * rows * BLOCK * BLOCK * RING**2 * groups
    return pl.pallas_call(
        functools.partial(multiply_kernel, prepare, len(operands)),
        out_shape=shapes,
        in_specs=[pl.BlockSpec(memory_space=pltpu.SMEM)] + [VMEM] * (len(operands) + 1),
        out_specs=[VMEM] * len(shapes),
        compiler_params=pltpu.CompilerParams(vmem_limit_bytes=GRANT),
        cost_estimate=pl.CostEstimate(
            flops=flops, bytes_accessed=2**20, transcendentals=0
        ),
    )(order, *operands, weights)


def to_cores(theirs, ours):
    arrived = [swap_cores(theirs[d]) for d in SENT]
    return {d: summed([ours[d], got]).astype(BF16) for d, got in zip(SENT, arrived)}


def along_first(mine):
    got = [lax.ppermute(mine[d], BOND, shifts(d, 0)) for d in (2, 1, 3)]
    return summed([mine[0], *got]).astype(BF16)


def along_second(pieces):
    got = [lax.ppermute(pieces[e], BOND, shifts(e, 1)) for e in (2, 1, 3)]
    return summed([pieces[0], *got]).astype(BF16)


def along_z(array):
    return [array] + [lax.ppermute(array, "z", ring_shift(d)) for d in (1, 2, 3)]


def mixing_kernel(place, near, operator_tensors, mixing):
    def iota(shape, dim):
        return lax.broadcasted_iota(jnp.int32, shape, dim)

    wide, tall = (ROWS, PHYSICAL * MPO_BOND), (MPO_BOND, ROWS)
    first = place[PLACE + 1] * MPO_BOND
    pick = (iota(wide, 1) == first + lax.rem(iota(wide, 0), MPO_BOND)).astype(BF16)
    spread = (iota(tall, 0) == lax.rem(iota(tall, 1), MPO_BOND)).astype(BF16)
    square = (ROWS, ROWS)
    same = lax.div(iota(square, 0), MPO_BOND) == lax.div(iota(square, 1), MPO_BOND)
    for site in range(SITE_COUNT):
        whole = operator_tensors[site].astype(F32)
        planes = [whole[:, number, :] for number in range(PHYSICAL)]
        for d in range(RING):
            turned = lax.rem(place[PLACE + 1] + RING - d, RING)
            weights = planes[0]
            for number in range(1, PHYSICAL):
                weights = jnp.where(turned == number, planes[number], weights)
            weights = weights.astype(BF16)
            narrow = lax.dot_general(
                pick, weights, (((1,), (1,)), ((), ())), preferred_element_type=F32
            ).astype(BF16)
            full = jnp.dot(narrow, spread, preferred_element_type=F32)
            mixing[site, d] = jnp.where(same, full, 0.0).astype(BF16)


def mixing_weights(operator_tensors, place, near):
    return pl.pallas_call(
        mixing_kernel,
        out_shape=jax.ShapeDtypeStruct((SITE_COUNT, RING, ROWS, ROWS), BF16),
        in_specs=[
            pl.BlockSpec(memory_space=pltpu.SMEM),
            pl.BlockSpec(memory_space=pl.ANY),
            VMEM,
        ],
        out_specs=VMEM,
        compiler_params=pltpu.CompilerParams(vmem_limit_bytes=8 * 2**20),
        cost_estimate=pl.CostEstimate(flops=10**9, bytes_accessed=10**6, transcendentals=0),
    )(place, near, jnp.swapaxes(operator_tensors, 1, 2))


def chosen_kernel(place, near, kept_columns, chosen):
    def iota(shape, dim):
        return lax.broadcasted_iota(jnp.int32, shape, dim)

    digits, wide = (16, kept_columns.shape[-1]), (16, BLOCK)
    high_of = lax.div(iota(wide, 1), 16) == iota(wide, 0)
    low_of = (lax.rem(iota(wide, 1), 16) == iota(wide, 0)).astype(F32)
    for site in range(SITE_COUNT):
        number = kept_columns[site : site + 1, :] - place[PLACE]
        here = (number >= 0) & (number < BLOCK * PHYSICAL) & (lax.rem(number, PHYSICAL) == place[PLACE + 1])
        column = jnp.where(here, lax.div(number, PHYSICAL), -1)
        high = (lax.div(column, 16) == iota(digits, 0)) & (column >= 0)
        low = lax.rem(column, 16) == iota(digits, 0)
        counts = lax.dot_general(
            high.astype(F32).astype(BF16),
            low.astype(F32).astype(BF16),
            (((1,), (1,)), ((), ())),
            preferred_element_type=F32,
        )
        spread = jnp.dot(counts, low_of, preferred_element_type=F32)
        total = jnp.sum(jnp.where(high_of, spread, 0.0), axis=0, keepdims=True)
        chosen[site] = (total > 0.5).astype(F32)


def chosen_columns(kept_columns, place, near):
    return pl.pallas_call(
        chosen_kernel,
        out_shape=jax.ShapeDtypeStruct((SITE_COUNT, 1, BLOCK), F32),
        in_specs=[
            pl.BlockSpec(memory_space=pltpu.SMEM),
            pl.BlockSpec(memory_space=pl.ANY),
            VMEM,
        ],
        out_specs=VMEM,
        compiler_params=pltpu.CompilerParams(vmem_limit_bytes=GRANT),
        cost_estimate=pl.CostEstimate(flops=10**8, bytes_accessed=10**5, transcendentals=0),
    )(place, near, kept_columns)


def chip_gram(grams):
    first = lax.axis_index("core") == 0
    got = swap_cores(jnp.where(first, grams[1], grams[0]))
    whole = summed([jnp.where(first, grams[0], grams[1]), got])
    whole = summed(along_z(whole.astype(BF16))).astype(BF16)
    return jnp.pad(whole, ((0, 0), (0, BLOCK - ROWS)))


def finish_kernel(core, own, other, grams, done):
    done[...] = jnp.zeros_like(done)
    mine, theirs = own[...], other[...]
    first = core[0] == 0
    grams[:, 0, :] = jnp.where(first, mine, theirs)
    grams[:, 1, :] = jnp.where(first, theirs, mine)


def state_kernel(after, a, b, c, d, state):
    state[...] = total(a, b, c, d).astype(BF16)


def last_state(parts, after):
    return pl.pallas_call(
        state_kernel,
        out_shape=jax.ShapeDtypeStruct((ROWS, BLOCK), BF16),
        in_specs=[pl.BlockSpec(memory_space=pl.ANY)] + [VMEM] * 4,
        out_specs=VMEM,
        compiler_params=pltpu.CompilerParams(vmem_limit_bytes=GRANT),
        cost_estimate=pl.CostEstimate(flops=10**5, bytes_accessed=10**5, transcendentals=0),
    )(after, *parts)


def both_grams(own):
    other = swap_cores(own)
    return pl.pallas_call(
        finish_kernel,
        out_shape=[
            jax.ShapeDtypeStruct((ROWS, SITE_COUNT, ROWS), F32),
            jax.ShapeDtypeStruct((8, 128), F32),
        ],
        in_specs=[pl.BlockSpec(memory_space=pltpu.SMEM)] + [VMEM] * 2,
        out_specs=[VMEM] * 2,
        compiler_params=pltpu.CompilerParams(vmem_limit_bytes=GRANT),
    )(lax.axis_index("core").astype(jnp.int32)[None], own, other)


def on_device(carried, site_tensors, operator_tensors, rotation, kept_columns):
    core = lax.axis_index("core")
    their_order, our_order = block_order(1 - core), block_order(core)
    own = jnp.stack([lax.axis_index(BOND) * BLOCK * PHYSICAL, lax.axis_index("z")])
    places = jnp.concatenate([their_order, our_order, own.astype(jnp.int32)])
    tensors = site_tensors.reshape(SITE_COUNT * BLOCK, BOND_DIM)
    turns = rotation.reshape(SITE_COUNT * BLOCK, BOND_DIM)
    grams, near, parts = [], None, None
    for site in range(SITE_COUNT):
        if near is None:
            pieces = multiply(None, [carried], places, load(site, tensors, places))
            theirs, ours = pieces[:RING], pieces[RING:]
        else:
            weights = load(site, tensors, near)
            state, *theirs = multiply(total, parts, their_order, weights)
            ours = multiply(None, [state], our_order, weights)
        mine = to_cores(theirs, ours)
        near = along_first(mine)
        if site == 0:
            mixing = mixing_weights(operator_tensors, places, mine[SENT[2]])
            chosen = chosen_columns(kept_columns, places, near)
        parts = along_z(along_second([near[e] for e in range(RING)]))
        weights = load(site, turns, near)
        mixed = [*parts, mixing[site], chosen[site]]
        kept, *theirs = multiply(mix, mixed, their_order, weights)
        grams.append(gram_of(kept))
        ours = multiply(None, [kept], our_order, weights)
        mine = to_cores(theirs, ours)
        near = along_first(mine)
        pieces = [near[e] for e in range(RING)]
        if site == SITE_COUNT - 1:
            gram = chip_gram(grams)
            both = along_second([jnp.stack([piece, gram]) for piece in pieces])
            parts, got = [both[0]], []
            for d in (2, 1, 3):
                got.append(lax.ppermute(both[1], BOND, shifts(d, 0)))
            for d in (2, 1, 3):
                parts.append(lax.ppermute(both[0], "z", ring_shift(d)))
            grams, done = both_grams(summed([both[1], *got])[:, :ROWS])
            return last_state(parts, done), jnp.swapaxes(grams, 0, 1)
        parts = along_z(along_second(pieces))


def solution(mesh):
    finer = Mesh(mesh.devices.reshape(RING, RING, 2, mesh.shape["mpo"]), (*BOND, "z"))
    placed = (P(None, BOND), P(None, BOND, "z", None), P(), P(None, BOND, "z", None), P())
    return jax.shard_map(
        on_device, mesh=finer, in_specs=placed, out_specs=(P(None, BOND), P()), check_vma=False
    )
```
